32 devices in a mesh: dp: 4 (over x, core), expert: 8 (over z, y).
Axes of the slice: x: 2, y: 2, z: 4, core: 2. Of those that a mesh axis runs over, the one named last changes fastest.
Arguments:
- tokens: bfloat16 [4096, 2048], P(('dp', 'expert')), may hold values from -6 to 6
- cotangent: bfloat16 [4096, 2048], P(('dp', 'expert')), may hold values from -6 to 6
- routes: int32 [4096, 3], P(('dp', 'expert')), may hold values from 0 to 7, all different within a row; in each aligned block of 128 rows (0 to 127, 128 to 255, ...) at most 60 rows name the same one
- gates: float32 [4096, 3], P(('dp', 'expert')), may hold values from 0.1 to 1
- gate_proj: bfloat16 [8, 768, 2048], P('expert'), may hold values from -0.125 to 0.125
- up_proj: bfloat16 [8, 768, 2048], P('expert'), may hold values from -0.125 to 0.125
- down_proj: bfloat16 [8, 768, 2048], P('expert'), may hold values from -0.21875 to 0.21875
Outputs:
- grad_tokens: bfloat16 [4096, 2048], P(('dp', 'expert'))
- grad_gate: bfloat16 [8, 768, 2048], P('expert', 'dp')
- grad_up: bfloat16 [8, 768, 2048], P('expert', 'dp')
- grad_down: bfloat16 [8, 768, 2048], P('expert', 'dp')
The draws below stay inside these ranges and needn't reach their ends.
Inputs may be any that keep to these rules, and one draw needn't show every extreme that they name: `routes`: each row names 3 different experts. Among the 128 rows of one device, no expert is named more than 60 times, and in some devices' rows some expert is named exactly 60 times.
All inputs are finite; a program needn't handle non-finite values.
Results may differ from the reference program's by a relative error of at most 0.0089.
Values may be sent and summed in bfloat16 or wider, within the bound.
A program may use at most 128 MiB of HBM per device.

```python
import math
import jax
import jax.numpy as jnp
import numpy as np
from jax import lax

D = 2048
FF = 768
TOP = 3
TOK_DEV = 128
EXPERTS = 8
CAP = 60
TOKENS = 4096
N_DP = 4
N_EXPERT = 8


def shard_levels(stream_key, extent, pieces, least, top_value):
    level = 1.0
    for axis_at, shards_of in pieces:
        draws = jax.random.uniform(jax.random.fold_in(jax.random.fold_in(stream_key, 6), axis_at), (shards_of,), jnp.float32, least / len(pieces), top_value / len(pieces))
        level = level * jnp.repeat(jnp.exp(draws), extent[axis_at] // shards_of).reshape((-1,) + (1,) * (len(extent) - 1 - axis_at))
    return level


def shared_out(rng, own, number, rows, count, top, limit, skew):
    sequence = jax.random.permutation(rng, count)
    heavy_load, ordinary = shares(count, rows * top, limit, skew, True), shares(count, rows * top, limit, skew, False)
    places = jnp.arange(count)

    def named(sizes, turn):
        used = int((sizes > 0).sum())
        fixed = max(1, used // 4)
        moved = fixed + (places - fixed + turn * (used - fixed)) % max(1, count - fixed)
        return jnp.zeros((count,), jnp.int32).at[sequence[jnp.where(places < fixed, places, moved)]].set(jnp.asarray(sizes, jnp.int32))

    sizes = jnp.where(number % 4 == 0, named(heavy_load, number // 4), named(ordinary, number - number // 4 - 1))
    mixed = jax.random.permutation(jax.random.fold_in(own, 3), count)
    donor, sink = mixed[0:count // 2 * 2:2], mixed[1:count // 2 * 2:2]
    margin = jnp.minimum(sizes[donor] - 1, limit - sizes[sink]) // 2
    margin = jnp.where((donor == sequence[0]) | (sink == sequence[0]) | (sizes[sink] == 0), 0, jnp.maximum(margin, 0))
    moved = jax.random.randint(jax.random.fold_in(own, 4), (count // 2,), 0, 1 << 20) % (margin + 1)
    sizes = sizes.at[donor].add(-moved).at[sink].add(moved)
    items = jnp.searchsorted(jnp.cumsum(sizes), jnp.arange(rows * top), side="right").astype(jnp.int32)
    listing = items.reshape(top, rows).T
    listing = listing[jax.random.permutation(jax.random.fold_in(own, 1), rows)]
    turn = jax.random.randint(jax.random.fold_in(own, 2), (rows, 1), 0, top)
    return jnp.take_along_axis(listing, (jnp.arange(top)[None, :] + turn) % top, axis=1)


def shares(amount, total, limit, skew, full):
    portions = [(1 << 20) // math.isqrt(rank ** skew) + 1 for rank in range(1, amount + 1)]
    largest = limit if full else min(limit, max(-(-total // amount), total * portions[0] // sum(portions)))
    least = 1 if total - largest >= amount - 1 else 0
    given, rest = [largest] + [least] * (amount - 1), total - largest - least * (amount - 1)
    while rest > 0:
        candidates = [i for i in range(1, amount) if given[i] < largest] or [i for i in range(1, amount) if given[i] < limit]
        mass, budget = sum([portions[i] for i in candidates]), rest
        for i in candidates:
            addition = min(limit - given[i], max(1, budget * portions[i] // mass), rest)
            given[i] = given[i] + addition
            rest = rest - addition
    return np.array(given)


def normal_values(own_key, shape, deviation, limit, shards=(), held_as=jnp.bfloat16):
    entries = jax.random.normal(own_key, shape, jnp.float32) * deviation
    if len(shards) > 0:
        entries = shard_levels(own_key, shape, shards, -0.22, 0.18) * entries
    return jnp.clip(entries, min=-limit, max=limit).astype(held_as)


def setup_inputs(seed: int = 0) -> dict:
    seeds = jax.random.split(jax.random.key(seed), 8)
    tokens = normal_values(seeds[0], (TOKENS, D), 1.0, 6.0, ((0, 32),))
    cotangent = normal_values(seeds[1], (TOKENS, D), 1.0, 6.0, ((0, 32),))
    routes_keys = jax.random.split(jax.random.fold_in(seeds[2], 1), TOKENS // TOK_DEV)
    routes_turns = jax.random.permutation(jax.random.fold_in(seeds[2], 3), TOKENS // TOK_DEV)
    routes = jax.vmap(lambda own, number: shared_out(jax.random.fold_in(seeds[2], 2), own, number, TOK_DEV, EXPERTS, TOP, CAP, 2))(routes_keys, routes_turns).reshape((TOKENS, TOP))
    gates = jnp.clip(0.1 + 0.9 * jax.random.uniform(seeds[3], (TOKENS, TOP), jnp.float32) ** shard_levels(seeds[3], (TOKENS, TOP), ((0, 32),), -0.2, 0.2), 0.1, 1.0)
    gate_proj = normal_values(seeds[4], (EXPERTS, FF, D), D ** -0.5, 0.125, ((0, 8),))
    up_proj = normal_values(seeds[5], (EXPERTS, FF, D), D ** -0.5, 0.125, ((0, 8),))
    down_proj = normal_values(seeds[6], (EXPERTS, FF, D), FF ** -0.5, 0.21875, ((0, 8),))
    return dict(tokens=tokens, cotangent=cotangent, routes=routes, gates=gates, gate_proj=gate_proj, up_proj=up_proj, down_proj=down_proj)


def expert_grads(rows_in, rows_grad, w_gate, w_up, w_down):
    gate_pre = jnp.dot(rows_in, w_gate.T, preferred_element_type=jnp.float32)
    up_pre = jnp.dot(rows_in, w_up.T, preferred_element_type=jnp.float32)
    sigma = jax.nn.sigmoid(gate_pre)
    active = gate_pre * sigma
    hidden = (active * up_pre).astype(jnp.bfloat16)
    grad_down = jnp.dot(hidden.T, rows_grad, preferred_element_type=jnp.float32)
    d_hidden = jnp.dot(rows_grad, w_down.T, preferred_element_type=jnp.float32)
    d_up = (d_hidden * active).astype(jnp.bfloat16)
    d_gate = (d_hidden * up_pre * sigma * (1.0 + gate_pre * (1.0 - sigma))).astype(jnp.bfloat16)
    grad_gate = jnp.dot(d_gate.T, rows_in, preferred_element_type=jnp.float32)
    grad_up = jnp.dot(d_up.T, rows_in, preferred_element_type=jnp.float32)
    d_assign = jnp.dot(d_gate, w_gate, preferred_element_type=jnp.float32) + jnp.dot(d_up, w_up, preferred_element_type=jnp.float32)
    return d_assign, grad_gate, grad_up, grad_down


def reference(tokens, cotangent, routes, gates, gate_proj, up_proj, down_proj):
    devices_all = N_DP * N_EXPERT
    per_device = TOK_DEV * TOP
    total = devices_all * per_device
    routes_flat = routes.reshape(devices_all, per_device)
    expert_ids = jnp.arange(EXPERTS, dtype=jnp.int32)
    onehot = (routes_flat[:, :, None] == expert_ids[None, None, :]).astype(jnp.int32)
    slot_index = jnp.sum((jnp.cumsum(onehot, axis=1) - onehot) * onehot, axis=2)
    device_ids = jnp.arange(devices_all, dtype=jnp.int32)[:, None]
    position = (device_ids * CAP + slot_index).reshape(-1).astype(jnp.int32)
    assign_ids = jnp.arange(total, dtype=jnp.int32)
    table = jnp.full((EXPERTS, devices_all * CAP), total, jnp.int32)
    table = table.at[routes_flat.reshape(-1).astype(jnp.int32), position].set(assign_ids)
    token_rows = jnp.concatenate([tokens, jnp.zeros((1, D), tokens.dtype)], axis=0)
    grad_rows = jnp.concatenate([cotangent, jnp.zeros((1, D), cotangent.dtype)], axis=0)
    gate_flat = jnp.concatenate([gates.reshape(-1), jnp.zeros((1,), gates.dtype)], axis=0)

    def step(accum, items):
        index, w_gate, w_up, w_down = items
        token_index = (index // TOP).astype(jnp.int32)
        rows_in = token_rows[token_index]
        rows_grad = (gate_flat[index][:, None] * grad_rows[token_index].astype(jnp.float32)).astype(jnp.bfloat16)
        d_assign, grad_gate, grad_up, grad_down = expert_grads(rows_in, rows_grad, w_gate, w_up, w_down)
        accum = accum.at[token_index].add(d_assign)
        return accum, (grad_gate.astype(jnp.bfloat16), grad_up.astype(jnp.bfloat16), grad_down.astype(jnp.bfloat16))

    start = jnp.zeros((TOKENS + 1, D), jnp.float32)
    accum, grads = lax.scan(step, start, (table, gate_proj, up_proj, down_proj))
    grad_tokens = accum[:TOKENS].astype(jnp.bfloat16)
    return grad_tokens, grads[0], grads[1], grads[2]
```

```python
import functools

import jax
import jax.numpy as jnp
from jax import lax
from jax.experimental import pallas as pl
from jax.experimental.pallas import tpu as pltpu
from jax.sharding import PartitionSpec as P


def expert_pass(rows_in, rows_grad, w_gate, w_up, w_down):
    gate_pre = jnp.einsum("rd,fd->rf", rows_in, w_gate, preferred_element_type=jnp.float32)
    up_pre = jnp.einsum("rd,fd->rf", rows_in, w_up, preferred_element_type=jnp.float32)
    sigma = jax.nn.sigmoid(gate_pre)
    active = gate_pre * sigma
    hidden = (active * up_pre).astype(jnp.bfloat16)
    grad_down = jnp.einsum("rf,rd->fd", hidden, rows_grad, preferred_element_type=jnp.float32)
    d_hidden = jnp.einsum("rd,fd->rf", rows_grad, w_down, preferred_element_type=jnp.float32)
    d_up = (d_hidden * active).astype(jnp.bfloat16)
    d_gate = (d_hidden * up_pre * sigma * (1.0 + gate_pre * (1.0 - sigma))).astype(jnp.bfloat16)
    grad_gate = jnp.einsum("rf,rd->fd", d_gate, rows_in, preferred_element_type=jnp.float32)
    grad_up = jnp.einsum("rf,rd->fd", d_up, rows_in, preferred_element_type=jnp.float32)
    d_assign = jnp.dot(d_gate, w_gate, preferred_element_type=jnp.float32) + jnp.dot(
        d_up, w_up, preferred_element_type=jnp.float32
    )
    return (d_assign, grad_gate, grad_up, grad_down)


def shards(tokens, cotangent, routes, gates, gate_proj, up_proj, down_proj):
    experts = lax.axis_size("expert")
    tok_count = tokens.shape[0]
    feature = tokens.shape[1]
    chosen = routes.shape[1]
    capacity = max(2, min(tok_count, 5 * tok_count * chosen // (4 * experts)))
    routes_flat = routes.reshape(-1)
    onehot = (routes_flat[:, None] == jnp.arange(experts, dtype=jnp.int32)[None, :]).astype(
        jnp.int32
    )
    slot_index = jnp.sum((jnp.cumsum(onehot, axis=0) - onehot) * onehot, axis=1)
    target = routes_flat * capacity + slot_index
    placing = (jnp.arange(experts * capacity, dtype=jnp.int32)[:, None] == target[None, :]).astype(
        jnp.bfloat16
    )
    scaled = (
        gates.reshape(-1)[:, None] * jnp.repeat(cotangent, chosen, axis=0).astype(jnp.float32)
    ).astype(jnp.bfloat16)
    stacked = jnp.concatenate([jnp.repeat(tokens, chosen, axis=0), scaled], axis=1)
    packed = jnp.dot(placing, stacked, preferred_element_type=jnp.float32).astype(jnp.bfloat16)
    sent_tokens = packed[:, :feature].reshape(experts, capacity, feature)
    sent_grads = packed[:, feature:].reshape(experts, capacity, feature)
    arrived = (
        lax.all_to_all(sent_tokens, "expert", split_axis=0, concat_axis=0, tiled=True),
        lax.all_to_all(sent_grads, "expert", split_axis=0, concat_axis=0, tiled=True),
    )
    d_assign, whole_gate, whole_up, whole_down = expert_pass(
        arrived[0].reshape(-1, feature),
        arrived[1].reshape(-1, feature),
        gate_proj[0],
        up_proj[0],
        down_proj[0],
    )
    reduced = d_assign.reshape(experts, capacity, feature)
    grad_gate, grad_up, grad_down = (
        lax.psum_scatter(whole_gate, "dp", scatter_dimension=0, tiled=True),
        lax.psum_scatter(whole_up, "dp", scatter_dimension=0, tiled=True),
        lax.psum_scatter(whole_down, "dp", scatter_dimension=0, tiled=True),
    )
    summed = lax.all_to_all(reduced, "expert", split_axis=0, concat_axis=0, tiled=True)
    picked = jnp.take(summed.reshape(experts * capacity, feature), target, axis=0)
    grad_tokens = jnp.sum(picked.reshape(tok_count, chosen, feature), axis=1).astype(jnp.bfloat16)
    return (
        grad_tokens,
        grad_gate.astype(jnp.bfloat16)[None],
        grad_up.astype(jnp.bfloat16)[None],
        grad_down.astype(jnp.bfloat16)[None],
    )


NT = (((1,), (1,)), ((), ()))
TN = (((0,), (0,)), ((), ()))


def flip(index, offset, count):
    total, bit = 0, 1
    while bit < count:
        total = total + ((index // bit) % 2 + (offset // bit) % 2) % 2 * bit
        bit *= 2
    return total


def layer_kernel(
    experts, cap, group, tok_ref, grd_ref, wg_hbm, wu_hbm, wd_hbm,
    ret_ref, og_ref, ou_ref, od_ref,
    rows, grads, wg, wu, wd, gate, up, hid, dgate, dup, dass,
    core_out, core_in, x_out, x_in, own,
    w_sem, loc_sem, tok_s, tok_r, grd_s, grd_r, ret_s, ret_r, core_s, core_r, x_s, x_r,
):
    me = lax.axis_index("expert")
    rank = lax.axis_index("dp")
    half, side = rank // 2, rank % 2
    core_peer = half * 2 + (1 - side)
    x_peer = (1 - half) * 2 + side
    ff, feature = wg.shape
    share = ff // 4
    f32, bf16 = jnp.float32, jnp.bfloat16

    loads = [
        pltpu.make_async_copy(a, b, w_sem.at[i])
        for i, (a, b) in enumerate(((wg_hbm, wg), (wu_hbm, wu), (wd_hbm, wd)))
    ]
    for c in loads:
        c.start()
    mine = [
        pltpu.make_async_copy(tok_ref.at[me], rows.at[pl.ds(0, cap)], loc_sem.at[0]),
        pltpu.make_async_copy(grd_ref.at[me], grads.at[pl.ds(0, cap)], loc_sem.at[1]),
    ]
    for c in mine:
        c.start()

    barrier = pltpu.get_barrier_semaphore()
    for d in range(1, experts):
        pl.semaphore_signal(barrier, inc=1, device_id={"expert": flip(me, d, experts)}, device_id_type=pl.DeviceIdType.MESH)
    for p in (core_peer, x_peer):
        pl.semaphore_signal(barrier, inc=1, device_id={"dp": p}, device_id_type=pl.DeviceIdType.MESH)
    pl.semaphore_wait(barrier, experts + 1)

    def to_expert(src, dst, s, r, d):
        return pltpu.make_async_remote_copy(
            src_ref=src, dst_ref=dst, send_sem=s.at[d], recv_sem=r.at[d],
            device_id={"expert": flip(me, d, experts)}, device_id_type=pl.DeviceIdType.MESH,
        )

    near = list(range(1, experts // 2))
    far = list(range(experts // 2, experts))
    tok_c, grd_c = {}, {}
    for d in far + near:
        tok_c[d] = to_expert(tok_ref.at[flip(me, d, experts)], rows.at[pl.ds(d * cap, cap)], tok_s, tok_r, d)
        tok_c[d].start()
    for d in near + far:
        grd_c[d] = to_expert(grd_ref.at[flip(me, d, experts)], grads.at[pl.ds(d * cap, cap)], grd_s, grd_r, d)
        grd_c[d].start()

    tile = ff // 2

    def forward(g):
        span = pl.ds(g * group, group)

        @pl.loop(0, 2)
        def _(t):
            part = pl.ds(pl.multiple_of(t * tile, tile), tile)
            x = rows[span, :]
            gp = lax.dot_general(wg[part, :], x, NT, preferred_element_type=f32)
            u = lax.dot_general(wu[part, :], x, NT, preferred_element_type=f32)
            gate[part, span] = gp
            up[part, span] = u
            hid[part, span] = (gp * jax.nn.sigmoid(gp) * u).astype(bf16)

    def backward(g):
        span = pl.ds(g * group, group)

        @pl.loop(0, 2)
        def _(t):
            part = pl.ds(pl.multiple_of(t * tile, tile), tile)
            dh = lax.dot_general(wd[part, :], grads[span, :], NT, preferred_element_type=f32)
            gp = gate[part, span]
            s = jax.nn.sigmoid(gp)
            dup[part, span] = (dh * (gp * s)).astype(bf16)
            dgate[part, span] = (dh * up[part, span] * s * (1.0 + gp * (1.0 - s))).astype(bf16)

    wide = feature // 4

    def assign(g):
        span = pl.ds(g * group, group)

        @pl.loop(0, 4)
        def _(t):
            cols = pl.ds(pl.multiple_of(t * wide, wide), wide)
            v = lax.dot_general(dgate[:, span], wg[:, cols], TN, preferred_element_type=f32)
            v += lax.dot_general(dup[:, span], wu[:, cols], TN, preferred_element_type=f32)
            dass[span, cols] = v.astype(bf16)

    def weight_grad(a, j, store):
        left = (dgate, dup, hid)[a]
        right = (rows, rows, grads)[a]
        part = pl.ds(pl.multiple_of(j * share, share), share)

        @pl.loop(0, 4)
        def _(t):
            cols = pl.ds(pl.multiple_of(t * wide, wide), wide)
            store(cols, jnp.dot(left[part, :], right[:, cols], preferred_element_type=f32))

    for c in loads[:2]:
        c.wait()
    mine[0].wait()
    for d in near:
        tok_c[d].wait_recv()
    forward(0)
    for d in far:
        tok_c[d].wait_recv()
    forward(1)
    loads[2].wait()
    mine[1].wait()
    for d in near:
        grd_c[d].wait_recv()
    backward(0)
    assign(0)
    ret_c = {}
    own_back = pltpu.make_async_copy(dass.at[pl.ds(0, cap)], ret_ref.at[me], loc_sem.at[0])
    own_back.start()
    for d in near:
        ret_c[d] = to_expert(dass.at[pl.ds(d * cap, cap)], ret_ref.at[me], ret_s, ret_r, d)
        ret_c[d].start()
    for d in far:
        grd_c[d].wait_recv()
    backward(1)

    core_c = {}

    def send_core(k, a, j):
        def store(cols, v):
            core_out[k * 3 + a, :, cols] = v.astype(bf16)

        weight_grad(a, j, store)
        core_c[k, a] = pltpu.make_async_remote_copy(
            src_ref=core_out.at[k * 3 + a], dst_ref=core_in.at[k * 3 + a],
            send_sem=core_s.at[k * 3 + a], recv_sem=core_r.at[k * 3 + a],
            device_id={"dp": core_peer}, device_id_type=pl.DeviceIdType.MESH,
        )
        core_c[k, a].start()

    for a in range(3):
        send_core(0, a, (1 - half) * 2 + (1 - side))
    assign(1)
    for d in far:
        ret_c[d] = to_expert(dass.at[pl.ds(d * cap, cap)], ret_ref.at[me], ret_s, ret_r, d)
        ret_c[d].start()
    x_c = {}
    for a in range(3):
        core_c[0, a].wait_recv()

        def store(cols, v, a=a):
            x_out[a, :, cols] = (v + core_in[a, :, cols].astype(f32)).astype(bf16)

        weight_grad(a, (1 - half) * 2 + side, store)
        x_c[a] = pltpu.make_async_remote_copy(
            src_ref=x_out.at[a], dst_ref=x_in.at[a], send_sem=x_s.at[a], recv_sem=x_r.at[a],
            device_id={"dp": x_peer}, device_id_type=pl.DeviceIdType.MESH,
        )
        x_c[a].start()
    for a in range(3):
        send_core(1, a, half * 2 + (1 - side))
    for a in range(3):
        core_c[1, a].wait_recv()

        def store(cols, v, a=a):
            own[a, :, cols] = v + core_in[3 + a, :, cols].astype(f32)

        weight_grad(a, half * 2 + side, store)
    for a, out in enumerate((og_ref, ou_ref, od_ref)):
        x_c[a].wait_recv()

        @pl.loop(0, 4)
        def _(t, a=a, out=out):
            cols = pl.ds(pl.multiple_of(t * wide, wide), wide)
            out[:, cols] = (own[a, :, cols] + x_in[a, :, cols].astype(f32)).astype(bf16)

    own_back.wait()
    for d in range(1, experts):
        ret_c[d].wait_recv()
        tok_c[d].wait_send()
        grd_c[d].wait_send()
        ret_c[d].wait_send()
    for c in core_c.values():
        c.wait_send()
    for c in x_c.values():
        c.wait_send()


def gathered(tokens, cotangent, routes, gates, gate_proj, up_proj, down_proj):
    experts = lax.axis_size("expert")
    tok_count, feature = tokens.shape
    chosen = routes.shape[1]
    ff = gate_proj.shape[1]
    capacity = max(2, min(tok_count, 5 * tok_count * chosen // (4 * experts)))
    cap = -(-capacity // 16) * 16
    f32, bf16 = jnp.float32, jnp.bfloat16
    hit = routes[:, :, None] == jnp.arange(experts, dtype=jnp.int32)[None, None, :]
    member = jnp.any(hit, axis=1)
    weight = jnp.sum(jnp.where(hit, gates[:, :, None], 0.0), axis=1)
    at = jnp.arange(tok_count, dtype=jnp.int32)
    earlier = (at[None, :] < at[:, None]).astype(bf16)
    slot = jnp.dot(earlier, member.astype(bf16), preferred_element_type=f32).astype(jnp.int32)
    slot = jnp.where(member, slot, cap)
    picks = slot.T[:, None, :] == jnp.arange(cap, dtype=jnp.int32)[None, :, None]
    placing = picks.reshape(experts * cap, tok_count).astype(bf16)
    factor = jnp.sum(jnp.where(picks, weight.T[:, None, :], 0.0), axis=2).reshape(-1, 1)
    packed = jnp.dot(placing, tokens, preferred_element_type=f32).astype(bf16)
    packed_grads = (factor * jnp.dot(placing, cotangent, preferred_element_type=f32)).astype(bf16)
    group = experts * cap // 2
    share = ff // 4
    rows = experts * cap
    vm = pl.BlockSpec(memory_space=pltpu.VMEM)
    anyspec = pl.BlockSpec(memory_space=pl.ANY)
    sem = pltpu.SemaphoreType.DMA
    back, grad_gate, grad_up, grad_down = pl.pallas_call(
        functools.partial(layer_kernel, experts, cap, group),
        out_shape=[jax.ShapeDtypeStruct((experts, cap, feature), bf16)]
        + [jax.ShapeDtypeStruct((share, feature), bf16)] * 3,
        in_specs=[vm, vm, anyspec, anyspec, anyspec],
        out_specs=[vm] * 4,
        scratch_shapes=[
            pltpu.VMEM((rows, feature), bf16),
            pltpu.VMEM((rows, feature), bf16),
            pltpu.VMEM((ff, feature), bf16),
            pltpu.VMEM((ff, feature), bf16),
            pltpu.VMEM((ff, feature), bf16),
            pltpu.VMEM((ff, rows), f32),
            pltpu.VMEM((ff, rows), f32),
            pltpu.VMEM((ff, rows), bf16),
            pltpu.VMEM((ff, rows), bf16),
            pltpu.VMEM((ff, rows), bf16),
            pltpu.VMEM((rows, feature), bf16),
            pltpu.VMEM((6, share, feature), bf16),
            pltpu.VMEM((6, share, feature), bf16),
            pltpu.VMEM((3, share, feature), bf16),
            pltpu.VMEM((3, share, feature), bf16),
            pltpu.VMEM((3, share, feature), f32),
            sem((3,)), sem((2,)),
            sem((experts,)), sem((experts,)), sem((experts,)), sem((experts,)),
            sem((experts,)), sem((experts,)),
            sem((6,)), sem((6,)), sem((3,)), sem((3,)),
        ],
        compiler_params=pltpu.CompilerParams(
            collective_id=0, has_side_effects=True, vmem_limit_bytes=64 * 1024 * 1024 - 65536
        ),
    )(
        packed.reshape(experts, cap, feature),
        packed_grads.reshape(experts, cap, feature),
        gate_proj[0], up_proj[0], down_proj[0],
    )
    grad_tokens = lax.dot_general(
        placing, back.reshape(rows, feature), TN, preferred_element_type=f32
    ).astype(bf16)
    return grad_tokens, grad_gate[None], grad_up[None], grad_down[None]


def fits(mesh):
    experts, replicas = mesh.shape["expert"], mesh.shape["dp"]
    return replicas == 4 and experts & (experts - 1) == 0 and experts <= 2 * replicas


def solution(mesh):
    return jax.shard_map(
        gathered if fits(mesh) else shards,
        mesh=mesh,
        in_specs=(
            P(("dp", "expert"), None),
            P(("dp", "expert"), None),
            P(("dp", "expert"), None),
            P(("dp", "expert"), None),
            P("expert", None, None),
            P("expert", None, None),
            P("expert", None, None),
        ),
        out_specs=(
            P(("dp", "expert"), None),
            P("expert", "dp", None),
            P("expert", "dp", None),
            P("expert", "dp", None),
        ),
        check_vma=False,
    )
```

```python
import functools

import jax
import jax.numpy as jnp
from jax import lax
from jax.experimental import pallas as pl
from jax.experimental.pallas import tpu as pltpu
from jax.sharding import PartitionSpec as P


def expert_pass(rows_in, rows_grad, w_gate, w_up, w_down):
    gate_pre = jnp.einsum("rd,fd->rf", rows_in, w_gate, preferred_element_type=jnp.float32)
    up_pre = jnp.einsum("rd,fd->rf", rows_in, w_up, preferred_element_type=jnp.float32)
    sigma = jax.nn.sigmoid(gate_pre)
    active = gate_pre * sigma
    hidden = (active * up_pre).astype(jnp.bfloat16)
    grad_down = jnp.einsum("rf,rd->fd", hidden, rows_grad, preferred_element_type=jnp.float32)
    d_hidden = jnp.einsum("rd,fd->rf", rows_grad, w_down, preferred_element_type=jnp.float32)
    d_up = (d_hidden * active).astype(jnp.bfloat16)
    d_gate = (d_hidden * up_pre * sigma * (1.0 + gate_pre * (1.0 - sigma))).astype(jnp.bfloat16)
    grad_gate = jnp.einsum("rf,rd->fd", d_gate, rows_in, preferred_element_type=jnp.float32)
    grad_up = jnp.einsum("rf,rd->fd", d_up, rows_in, preferred_element_type=jnp.float32)
    d_assign = jnp.dot(d_gate, w_gate, preferred_element_type=jnp.float32) + jnp.dot(
        d_up, w_up, preferred_element_type=jnp.float32
    )
    return (d_assign, grad_gate, grad_up, grad_down)


def shards(tokens, cotangent, routes, gates, gate_proj, up_proj, down_proj):
    experts = lax.axis_size("expert")
    tok_count = tokens.shape[0]
    feature = tokens.shape[1]
    chosen = routes.shape[1]
    capacity = max(2, min(tok_count, 5 * tok_count * chosen // (4 * experts)))
    routes_flat = routes.reshape(-1)
    onehot = (routes_flat[:, None] == jnp.arange(experts, dtype=jnp.int32)[None, :]).astype(
        jnp.int32
    )
    slot_index = jnp.sum((jnp.cumsum(onehot, axis=0) - onehot) * onehot, axis=1)
    target = routes_flat * capacity + slot_index
    placing = (jnp.arange(experts * capacity, dtype=jnp.int32)[:, None] == target[None, :]).astype(
        jnp.bfloat16
    )
    scaled = (
        gates.reshape(-1)[:, None] * jnp.repeat(cotangent, chosen, axis=0).astype(jnp.float32)
    ).astype(jnp.bfloat16)
    stacked = jnp.concatenate([jnp.repeat(tokens, chosen, axis=0), scaled], axis=1)
    packed = jnp.dot(placing, stacked, preferred_element_type=jnp.float32).astype(jnp.bfloat16)
    sent_tokens = packed[:, :feature].reshape(experts, capacity, feature)
    sent_grads = packed[:, feature:].reshape(experts, capacity, feature)
    arrived = (
        lax.all_to_all(sent_tokens, "expert", split_axis=0, concat_axis=0, tiled=True),
        lax.all_to_all(sent_grads, "expert", split_axis=0, concat_axis=0, tiled=True),
    )
    d_assign, whole_gate, whole_up, whole_down = expert_pass(
        arrived[0].reshape(-1, feature),
        arrived[1].reshape(-1, feature),
        gate_proj[0],
        up_proj[0],
        down_proj[0],
    )
    reduced = d_assign.reshape(experts, capacity, feature)
    grad_gate, grad_up, grad_down = (
        lax.psum_scatter(whole_gate, "dp", scatter_dimension=0, tiled=True),
        lax.psum_scatter(whole_up, "dp", scatter_dimension=0, tiled=True),
        lax.psum_scatter(whole_down, "dp", scatter_dimension=0, tiled=True),
    )
    summed = lax.all_to_all(reduced, "expert", split_axis=0, concat_axis=0, tiled=True)
    picked = jnp.take(summed.reshape(experts * capacity, feature), target, axis=0)
    grad_tokens = jnp.sum(picked.reshape(tok_count, chosen, feature), axis=1).astype(jnp.bfloat16)
    return (
        grad_tokens,
        grad_gate.astype(jnp.bfloat16)[None],
        grad_up.astype(jnp.bfloat16)[None],
        grad_down.astype(jnp.bfloat16)[None],
    )


NT = (((1,), (1,)), ((), ()))
TN = (((0,), (0,)), ((), ()))


def flip(index, offset, count):
    total, bit = 0, 1
    while bit < count:
        total = total + ((index // bit) % 2 + (offset // bit) % 2) % 2 * bit
        bit *= 2
    return total


def layer_kernel(
    experts, cap, group, all_tok, all_cot, info_ref, tok_ref, grd_ref, wg_hbm, wu_hbm, wd_hbm,
    ret_ref, part_in, og_ref, ou_ref, od_ref,
    rows, grads, wg, wu, wd, gate, up, hid, dgate, dup, dass,
    far_tok, far_cot, far_info, chosen, pack_tok, pack_grd, relay_in, part_out,
    core_out, core_in, x_out, x_in, own,
    w_sem, loc_sem, far_s, far_r, tok_s, tok_r, grd_s, grd_r, ret_s, ret_r, core_s, core_r, x_s, x_r,
):
    me = lax.axis_index("expert")
    rank = lax.axis_index("dp")
    half, side = rank // 2, rank % 2
    core_peer = half * 2 + (1 - side)
    x_peer = (1 - half) * 2 + side
    ff, feature = wg.shape
    share = ff // 4
    f32, bf16 = jnp.float32, jnp.bfloat16

    loads = [
        pltpu.make_async_copy(a, b, w_sem.at[i])
        for i, (a, b) in enumerate(((wg_hbm, wg), (wu_hbm, wu), (wd_hbm, wd)))
    ]
    for c in loads:
        c.start()
    mine = [
        pltpu.make_async_copy(tok_ref.at[pl.ds(0, cap)], rows.at[pl.ds(0, cap)], loc_sem.at[0]),
        pltpu.make_async_copy(grd_ref.at[pl.ds(0, cap)], grads.at[pl.ds(0, cap)], loc_sem.at[1]),
    ]
    for c in mine:
        c.start()

    barrier = pltpu.get_barrier_semaphore()
    near = experts // 2
    peers = list(range(1, near))
    for d in peers + [near]:
        pl.semaphore_signal(barrier, inc=1, device_id={"expert": flip(me, d, experts)}, device_id_type=pl.DeviceIdType.MESH)
    for p in (core_peer, x_peer):
        pl.semaphore_signal(barrier, inc=1, device_id={"dp": p}, device_id_type=pl.DeviceIdType.MESH)
    pl.semaphore_wait(barrier, near + 2)

    def to_expert(src, dst, s, r, at, d):
        copy = pltpu.make_async_remote_copy(
            src_ref=src, dst_ref=dst, send_sem=s.at[at], recv_sem=r.at[at],
            device_id={"expert": flip(me, d, experts)}, device_id_type=pl.DeviceIdType.MESH,
        )
        copy.start()
        return copy

    def slots(d):
        return pl.ds(d * cap, cap)

    tok_c, grd_c, ret_c = {}, {}, {}
    info_c = to_expert(info_ref, far_info, far_s, far_r, 0, near)
    ftok_c = to_expert(all_tok, far_tok, far_s, far_r, 1, near)
    for q in peers:
        tok_c[q] = to_expert(tok_ref.at[slots(q)], rows.at[slots(q)], tok_s, tok_r, q, q)
    fcot_c = to_expert(all_cot, far_cot, far_s, far_r, 2, near)
    for q in peers:
        grd_c[q] = to_expert(grd_ref.at[slots(q)], grads.at[slots(q)], grd_s, grd_r, q, q)

    tile = ff // 2

    def forward(g):
        span = pl.ds(g * group, group)

        @pl.loop(0, 2)
        def _(t):
            part = pl.ds(pl.multiple_of(t * tile, tile), tile)
            x = rows[span, :]
            gp = lax.dot_general(wg[part, :], x, NT, preferred_element_type=f32)
            u = lax.dot_general(wu[part, :], x, NT, preferred_element_type=f32)
            gate[part, span] = gp
            up[part, span] = u
            hid[part, span] = (gp * jax.nn.sigmoid(gp) * u).astype(bf16)

    def backward(g):
        span = pl.ds(g * group, group)

        @pl.loop(0, 2)
        def _(t):
            part = pl.ds(pl.multiple_of(t * tile, tile), tile)
            dh = lax.dot_general(wd[part, :], grads[span, :], NT, preferred_element_type=f32)
            gp = gate[part, span]
            s = jax.nn.sigmoid(gp)
            dup[part, span] = (dh * (gp * s)).astype(bf16)
            dgate[part, span] = (dh * up[part, span] * s * (1.0 + gp * (1.0 - s))).astype(bf16)

    wide = feature // 4

    def assign(g):
        span = pl.ds(g * group, group)

        @pl.loop(0, 4)
        def _(t):
            cols = pl.ds(pl.multiple_of(t * wide, wide), wide)
            v = lax.dot_general(dgate[:, span], wg[:, cols], TN, preferred_element_type=f32)
            v += lax.dot_general(dup[:, span], wu[:, cols], TN, preferred_element_type=f32)
            dass[span, cols] = v.astype(bf16)

    def weight_grad(a, j, store):
        left = (dgate, dup, hid)[a]
        right = (rows, rows, grads)[a]
        part = pl.ds(pl.multiple_of(j * share, share), share)

        @pl.loop(0, 4)
        def _(t):
            cols = pl.ds(pl.multiple_of(t * wide, wide), wide)
            store(cols, jnp.dot(left[part, :], right[:, cols], preferred_element_type=f32))

    count = all_tok.shape[0]

    def picks(q):
        place = lax.broadcasted_iota(jnp.int32, (cap, count), 0).astype(f32)
        return place == far_info[q : q + 1, :]

    info_c.wait_recv()
    for q in range(near):
        chosen[slots(q), :] = jnp.where(picks(q), 1.0, 0.0).astype(bf16)
    ftok_c.wait_recv()
    for q in peers + [0]:
        packed = jnp.dot(chosen[slots(q), :], far_tok[...], preferred_element_type=f32).astype(bf16)
        if q == 0:
            rows[slots(near), :] = packed
        else:
            pack_tok[slots(q), :] = packed
            tok_c[near + q] = to_expert(
                pack_tok.at[slots(q)], rows.at[slots(near + q)], tok_s, tok_r, near + q, q
            )
    for c in loads[:2]:
        c.wait()
    mine[0].wait()
    for q in peers:
        tok_c[q].wait_recv()
    forward(0)
    fcot_c.wait_recv()
    for q in peers + [0]:
        factor = jnp.sum(
            jnp.where(picks(q), far_info[near + q : near + q + 1, :], 0.0), axis=1, keepdims=True
        )
        packed = jnp.dot(chosen[slots(q), :], far_cot[...], preferred_element_type=f32)
        packed = (factor * packed).astype(bf16)
        if q == 0:
            grads[slots(near), :] = packed
        else:
            pack_grd[slots(q), :] = packed
            grd_c[near + q] = to_expert(
                pack_grd.at[slots(q)], grads.at[slots(near + q)], grd_s, grd_r, near + q, q
            )
    loads[2].wait()
    mine[1].wait()
    for q in peers:
        grd_c[q].wait_recv()
    backward(0)
    assign(0)
    own_back = pltpu.make_async_copy(dass.at[slots(0)], ret_ref.at[slots(0)], loc_sem.at[0])
    own_back.start()
    for q in peers:
        ret_c[q] = to_expert(dass.at[slots(q)], ret_ref.at[slots(q)], ret_s, ret_r, q, q)
    for q in peers:
        tok_c[near + q].wait_recv()
    forward(1)
    for q in peers:
        grd_c[near + q].wait_recv()
    backward(1)

    core_c = {}

    def send_core(k, a, j):
        def store(cols, v):
            core_out[k * 3 + a, :, cols] = v.astype(bf16)

        weight_grad(a, j, store)
        core_c[k, a] = pltpu.make_async_remote_copy(
            src_ref=core_out.at[k * 3 + a], dst_ref=core_in.at[k * 3 + a],
            send_sem=core_s.at[k * 3 + a], recv_sem=core_r.at[k * 3 + a],
            device_id={"dp": core_peer}, device_id_type=pl.DeviceIdType.MESH,
        )
        core_c[k, a].start()

    for a in range(3):
        send_core(0, a, (1 - half) * 2 + (1 - side))
    assign(1)
    for q in peers:
        ret_c[near + q] = to_expert(
            dass.at[slots(near + q)], relay_in.at[slots(q)], ret_s, ret_r, near + q, q
        )
    relay_in[slots(0), :] = dass[slots(near), :]
    x_c = {}
    for a in range(3):
        core_c[0, a].wait_recv()

        def store(cols, v, a=a):
            x_out[a, :, cols] = (v + core_in[a, :, cols].astype(f32)).astype(bf16)

        weight_grad(a, (1 - half) * 2 + side, store)
        x_c[a] = pltpu.make_async_remote_copy(
            src_ref=x_out.at[a], dst_ref=x_in.at[a], send_sem=x_s.at[a], recv_sem=x_r.at[a],
            device_id={"dp": x_peer}, device_id_type=pl.DeviceIdType.MESH,
        )
        x_c[a].start()
    for a in range(3):
        send_core(1, a, half * 2 + (1 - side))
    for q in peers:
        ret_c[near + q].wait_recv()

    @pl.loop(0, 4)
    def _(t):
        cols = pl.ds(pl.multiple_of(t * wide, wide), wide)
        v = lax.dot_general(chosen[...], relay_in[:, cols], TN, preferred_element_type=f32)
        part_out[:, cols] = v.astype(bf16)

    part_c = to_expert(part_out, part_in, far_s, far_r, 3, near)
    for a in range(3):
        core_c[1, a].wait_recv()

        def store(cols, v, a=a):
            own[a, :, cols] = v + core_in[3 + a, :, cols].astype(f32)

        weight_grad(a, half * 2 + side, store)
    for a, out in enumerate((og_ref, ou_ref, od_ref)):
        x_c[a].wait_recv()

        @pl.loop(0, 4)
        def _(t, a=a, out=out):
            cols = pl.ds(pl.multiple_of(t * wide, wide), wide)
            out[:, cols] = (own[a, :, cols] + x_in[a, :, cols].astype(f32)).astype(bf16)

    own_back.wait()
    for q in peers:
        ret_c[q].wait_recv()
    part_c.wait_recv()
    for c in (info_c, ftok_c, fcot_c, part_c):
        c.wait_send()
    for d in tok_c:
        tok_c[d].wait_send()
        grd_c[d].wait_send()
        ret_c[d].wait_send()
    for c in core_c.values():
        c.wait_send()
    for c in x_c.values():
        c.wait_send()


def gathered(tokens, cotangent, routes, gates, gate_proj, up_proj, down_proj):
    experts = lax.axis_size("expert")
    tok_count, feature = tokens.shape
    chosen = routes.shape[1]
    ff = gate_proj.shape[1]
    capacity = max(2, min(tok_count, 5 * tok_count * chosen // (4 * experts)))
    cap = -(-capacity // 16) * 16
    f32, bf16 = jnp.float32, jnp.bfloat16
    near = experts // 2
    order = jnp.arange(experts, dtype=jnp.int32) ^ lax.axis_index("expert")
    hit = routes[:, :, None] == order[None, None, :]
    member = jnp.any(hit, axis=1)
    weight = jnp.sum(jnp.where(hit, gates[:, :, None], 0.0), axis=1)
    at = jnp.arange(tok_count, dtype=jnp.int32)
    earlier = (at[None, :] < at[:, None]).astype(bf16)
    slot = jnp.dot(earlier, member.astype(bf16), preferred_element_type=f32).astype(jnp.int32)
    slot = jnp.where(member, slot, cap)
    info = jnp.concatenate([slot.T[near:].astype(f32), weight.T[near:]], axis=0)
    picks = slot.T[:near, None, :] == jnp.arange(cap, dtype=jnp.int32)[None, :, None]
    placing = picks.reshape(near * cap, tok_count).astype(bf16)
    factor = jnp.sum(jnp.where(picks, weight.T[:near, None, :], 0.0), axis=2).reshape(-1, 1)
    packed = jnp.dot(placing, tokens, preferred_element_type=f32).astype(bf16)
    packed_grads = (factor * jnp.dot(placing, cotangent, preferred_element_type=f32)).astype(bf16)
    group = experts * cap // 2
    share = ff // 4
    rows = experts * cap
    vm = pl.BlockSpec(memory_space=pltpu.VMEM)
    anyspec = pl.BlockSpec(memory_space=pl.ANY)
    sem = pltpu.SemaphoreType.DMA
    back, part, grad_gate, grad_up, grad_down = pl.pallas_call(
        functools.partial(layer_kernel, experts, cap, group),
        out_shape=[
            jax.ShapeDtypeStruct((near * cap, feature), bf16),
            jax.ShapeDtypeStruct((tok_count, feature), bf16),
        ]
        + [jax.ShapeDtypeStruct((share, feature), bf16)] * 3,
        in_specs=[vm, vm, vm, vm, vm, anyspec, anyspec, anyspec],
        out_specs=[vm] * 5,
        scratch_shapes=[
            pltpu.VMEM((rows, feature), bf16),
            pltpu.VMEM((rows, feature), bf16),
            pltpu.VMEM((ff, feature), bf16),
            pltpu.VMEM((ff, feature), bf16),
            pltpu.VMEM((ff, feature), bf16),
            pltpu.VMEM((ff, rows), f32),
            pltpu.VMEM((ff, rows), f32),
            pltpu.VMEM((ff, rows), bf16),
            pltpu.VMEM((ff, rows), bf16),
            pltpu.VMEM((ff, rows), bf16),
            pltpu.VMEM((rows, feature), bf16),
            pltpu.VMEM((tok_count, feature), bf16),
            pltpu.VMEM((tok_count, feature), bf16),
            pltpu.VMEM((experts, tok_count), f32),
            pltpu.VMEM((near * cap, tok_count), bf16),
            pltpu.VMEM((near * cap, feature), bf16),
            pltpu.VMEM((near * cap, feature), bf16),
            pltpu.VMEM((near * cap, feature), bf16),
            pltpu.VMEM((tok_count, feature), bf16),
            pltpu.VMEM((6, share, feature), bf16),
            pltpu.VMEM((6, share, feature), bf16),
            pltpu.VMEM((3, share, feature), bf16),
            pltpu.VMEM((3, share, feature), bf16),
            pltpu.VMEM((3, share, feature), f32),
            sem((3,)), sem((2,)), sem((4,)), sem((4,)),
            sem((experts,)), sem((experts,)), sem((experts,)), sem((experts,)),
            sem((experts,)), sem((experts,)),
            sem((6,)), sem((6,)), sem((3,)), sem((3,)),
        ],
        compiler_params=pltpu.CompilerParams(
            collective_id=0, has_side_effects=True, vmem_limit_bytes=64 * 1024 * 1024 - 65536
        ),
    )(
        tokens, cotangent, info, packed, packed_grads,
        gate_proj[0], up_proj[0], down_proj[0],
    )
    grad_tokens = lax.dot_general(placing, back, TN, preferred_element_type=f32)
    grad_tokens = (grad_tokens + part.astype(f32)).astype(bf16)
    return grad_tokens, grad_gate[None], grad_up[None], grad_down[None]


def fits(mesh):
    experts, replicas = mesh.shape["expert"], mesh.shape["dp"]
    return replicas == 4 and experts & (experts - 1) == 0 and experts <= 2 * replicas


def solution(mesh):
    return jax.shard_map(
        gathered if fits(mesh) else shards,
        mesh=mesh,
        in_specs=(
            P(("dp", "expert"), None),
            P(("dp", "expert"), None),
            P(("dp", "expert"), None),
            P(("dp", "expert"), None),
            P("expert", None, None),
            P("expert", None, None),
            P("expert", None, None),
        ),
        out_specs=(
            P(("dp", "expert"), None),
            P("expert", "dp", None),
            P("expert", "dp", None),
            P("expert", "dp", None),
        ),
        check_vma=False,
    )
```

```python
import functools

import jax
import jax.numpy as jnp
from jax import lax
from jax.experimental import pallas as pl
from jax.experimental.pallas import tpu as pltpu
from jax.sharding import PartitionSpec as P


def expert_pass(rows_in, rows_grad, w_gate, w_up, w_down):
    gate_pre = jnp.einsum("rd,fd->rf", rows_in, w_gate, preferred_element_type=jnp.float32)
    up_pre = jnp.einsum("rd,fd->rf", rows_in, w_up, preferred_element_type=jnp.float32)
    sigma = jax.nn.sigmoid(gate_pre)
    active = gate_pre * sigma
    hidden = (active * up_pre).astype(jnp.bfloat16)
    grad_down = jnp.einsum("rf,rd->fd", hidden, rows_grad, preferred_element_type=jnp.float32)
    d_hidden = jnp.einsum("rd,fd->rf", rows_grad, w_down, preferred_element_type=jnp.float32)
    d_up = (d_hidden * active).astype(jnp.bfloat16)
    d_gate = (d_hidden * up_pre * sigma * (1.0 + gate_pre * (1.0 - sigma))).astype(jnp.bfloat16)
    grad_gate = jnp.einsum("rf,rd->fd", d_gate, rows_in, preferred_element_type=jnp.float32)
    grad_up = jnp.einsum("rf,rd->fd", d_up, rows_in, preferred_element_type=jnp.float32)
    d_assign = jnp.dot(d_gate, w_gate, preferred_element_type=jnp.float32) + jnp.dot(
        d_up, w_up, preferred_element_type=jnp.float32
    )
    return (d_assign, grad_gate, grad_up, grad_down)


def shards(tokens, cotangent, routes, gates, gate_proj, up_proj, down_proj):
    experts = lax.axis_size("expert")
    tok_count = tokens.shape[0]
    feature = tokens.shape[1]
    chosen = routes.shape[1]
    capacity = max(2, min(tok_count, 5 * tok_count * chosen // (4 * experts)))
    routes_flat = routes.reshape(-1)
    onehot = (routes_flat[:, None] == jnp.arange(experts, dtype=jnp.int32)[None, :]).astype(
        jnp.int32
    )
    slot_index = jnp.sum((jnp.cumsum(onehot, axis=0) - onehot) * onehot, axis=1)
    target = routes_flat * capacity + slot_index
    placing = (jnp.arange(experts * capacity, dtype=jnp.int32)[:, None] == target[None, :]).astype(
        jnp.bfloat16
    )
    scaled = (
        gates.reshape(-1)[:, None] * jnp.repeat(cotangent, chosen, axis=0).astype(jnp.float32)
    ).astype(jnp.bfloat16)
    stacked = jnp.concatenate([jnp.repeat(tokens, chosen, axis=0), scaled], axis=1)
    packed = jnp.dot(placing, stacked, preferred_element_type=jnp.float32).astype(jnp.bfloat16)
    sent_tokens = packed[:, :feature].reshape(experts, capacity, feature)
    sent_grads = packed[:, feature:].reshape(experts, capacity, feature)
    arrived = (
        lax.all_to_all(sent_tokens, "expert", split_axis=0, concat_axis=0, tiled=True),
        lax.all_to_all(sent_grads, "expert", split_axis=0, concat_axis=0, tiled=True),
    )
    d_assign, whole_gate, whole_up, whole_down = expert_pass(
        arrived[0].reshape(-1, feature),
        arrived[1].reshape(-1, feature),
        gate_proj[0],
        up_proj[0],
        down_proj[0],
    )
    reduced = d_assign.reshape(experts, capacity, feature)
    grad_gate, grad_up, grad_down = (
        lax.psum_scatter(whole_gate, "dp", scatter_dimension=0, tiled=True),
        lax.psum_scatter(whole_up, "dp", scatter_dimension=0, tiled=True),
        lax.psum_scatter(whole_down, "dp", scatter_dimension=0, tiled=True),
    )
    summed = lax.all_to_all(reduced, "expert", split_axis=0, concat_axis=0, tiled=True)
    picked = jnp.take(summed.reshape(experts * capacity, feature), target, axis=0)
    grad_tokens = jnp.sum(picked.reshape(tok_count, chosen, feature), axis=1).astype(jnp.bfloat16)
    return (
        grad_tokens,
        grad_gate.astype(jnp.bfloat16)[None],
        grad_up.astype(jnp.bfloat16)[None],
        grad_down.astype(jnp.bfloat16)[None],
    )


NT = (((1,), (1,)), ((), ()))
TN = (((0,), (0,)), ((), ()))


def flip(index, offset, count):
    total, bit = 0, 1
    while bit < count:
        total = total + ((index // bit) % 2 + (offset // bit) % 2) % 2 * bit
        bit *= 2
    return total


def layer_kernel(
    experts, cap, group, all_tok, all_cot, info_ref, wg_hbm, wu_hbm, wd_hbm,
    ret_ref, part_in, og_ref, ou_ref, od_ref,
    rows, grads, wg, wu, wd, gate, up, hid, dgate, dup, dass,
    far_tok, far_cot, far_info, chosen, mine, near_tok, near_grd, pack_tok, pack_grd, relay_in, part_out,
    core_out, core_in, x_out, x_in, own,
    w_sem, loc_sem, far_s, far_r, tok_s, tok_r, grd_s, grd_r, ret_s, ret_r, core_s, core_r, x_s, x_r,
):
    me = lax.axis_index("expert")
    rank = lax.axis_index("dp")
    half, side = rank // 2, rank % 2
    core_peer = half * 2 + (1 - side)
    x_peer = (1 - half) * 2 + side
    ff, feature = wg.shape
    share = ff // 4
    f32, bf16 = jnp.float32, jnp.bfloat16

    loads = [
        pltpu.make_async_copy(a, b, w_sem.at[i])
        for i, (a, b) in enumerate(((wg_hbm, wg), (wu_hbm, wu), (wd_hbm, wd)))
    ]
    for c in loads:
        c.start()
    barrier = pltpu.get_barrier_semaphore()
    near = experts // 2
    peers = list(range(1, near))
    for d in peers + [near]:
        pl.semaphore_signal(barrier, inc=1, device_id={"expert": flip(me, d, experts)}, device_id_type=pl.DeviceIdType.MESH)
    for p in (core_peer, x_peer):
        pl.semaphore_signal(barrier, inc=1, device_id={"dp": p}, device_id_type=pl.DeviceIdType.MESH)
    pl.semaphore_wait(barrier, near + 2)

    def to_expert(src, dst, s, r, at, d):
        copy = pltpu.make_async_remote_copy(
            src_ref=src, dst_ref=dst, send_sem=s.at[at], recv_sem=r.at[at],
            device_id={"expert": flip(me, d, experts)}, device_id_type=pl.DeviceIdType.MESH,
        )
        copy.start()
        return copy

    def slots(d):
        return pl.ds(d * cap, cap)

    tok_c, grd_c, ret_c, fcot_c = {}, {}, {}, {}
    count = all_tok.shape[0]
    wide = feature // 4
    steps = range(4)

    def columns(t):
        return pl.ds(t * wide, wide)

    def picks(table, q):
        place = lax.broadcasted_iota(jnp.int32, (cap, count), 0).astype(f32)
        return place == table[q : q + 1, :]

    def factors(table, first, weights):
        return jnp.concatenate(
            [
                jnp.sum(
                    jnp.where(picks(table, first + q), table[weights + q : weights + q + 1, :], 0.0),
                    axis=1,
                    keepdims=True,
                )
                for q in range(near)
            ],
            axis=0,
        )

    def far_send(t):
        fcot_c[t] = to_expert(
            all_cot.at[:, columns(t)], far_cot.at[:, columns(t)], far_s, far_r, 3 + t, near
        )

    def grad_send(source, base, t):
        for q in peers:
            grd_c[base + q, t] = to_expert(
                source.at[slots(q), columns(t)], grads.at[slots(base + q), columns(t)],
                grd_s, grd_r, (base + q) * 4 + t, q,
            )

    def pack_grads(sel, factor, source, out, base, t):
        v = jnp.dot(sel[...], source[:, columns(t)], preferred_element_type=f32)
        v = (factor * v).astype(bf16)
        out[:, columns(t)] = v
        grads[slots(base), columns(t)] = v[:cap]

    def pack_tokens(sel, source, out, base):
        for t in steps:
            v = jnp.dot(sel[...], source[:, columns(t)], preferred_element_type=f32).astype(bf16)
            out[:, columns(t)] = v
            rows[slots(base), columns(t)] = v[:cap]
        for q in peers:
            tok_c[base + q] = to_expert(
                out.at[slots(q)], rows.at[slots(base + q)], tok_s, tok_r, base + q, q
            )

    info_c = to_expert(info_ref, far_info, far_s, far_r, 0, near)
    ftok_c = to_expert(all_tok, far_tok, far_s, far_r, 1, near)
    for q in range(near):
        mine[slots(q), :] = jnp.where(picks(info_ref, q), 1.0, 0.0).astype(bf16)
    pack_tokens(mine, all_tok, near_tok, 0)
    far_send(0)
    far_send(1)
    near_factor = factors(info_ref, 0, experts)
    for t in steps:
        pack_grads(mine, near_factor, all_cot, near_grd, 0, t)

    tile = ff // 2

    def forward(g):
        span = pl.ds(g * group, group)

        @pl.loop(0, 2)
        def _(t):
            part = pl.ds(pl.multiple_of(t * tile, tile), tile)
            x = rows[span, :]
            gp = lax.dot_general(wg[part, :], x, NT, preferred_element_type=f32)
            u = lax.dot_general(wu[part, :], x, NT, preferred_element_type=f32)
            gate[part, span] = gp
            up[part, span] = u
            hid[part, span] = (gp * jax.nn.sigmoid(gp) * u).astype(bf16)

    def backward(g):
        span = pl.ds(g * group, group)

        @pl.loop(0, 2)
        def _(t):
            part = pl.ds(pl.multiple_of(t * tile, tile), tile)
            dh = lax.dot_general(wd[part, :], grads[span, :], NT, preferred_element_type=f32)
            gp = gate[part, span]
            s = jax.nn.sigmoid(gp)
            dup[part, span] = (dh * (gp * s)).astype(bf16)
            dgate[part, span] = (dh * up[part, span] * s * (1.0 + gp * (1.0 - s))).astype(bf16)

    def assign(g):
        span = pl.ds(g * group, group)

        @pl.loop(0, 4)
        def _(t):
            cols = pl.ds(pl.multiple_of(t * wide, wide), wide)
            v = lax.dot_general(dgate[:, span], wg[:, cols], TN, preferred_element_type=f32)
            v += lax.dot_general(dup[:, span], wu[:, cols], TN, preferred_element_type=f32)
            dass[span, cols] = v.astype(bf16)

    def weight_grad(a, j, store):
        left = (dgate, dup, hid)[a]
        right = (rows, rows, grads)[a]
        part = pl.ds(pl.multiple_of(j * share, share), share)

        @pl.loop(0, 4)
        def _(t):
            cols = pl.ds(pl.multiple_of(t * wide, wide), wide)
            store(cols, jnp.dot(left[part, :], right[:, cols], preferred_element_type=f32))

    info_c.wait_recv()
    for q in range(near):
        chosen[slots(q), :] = jnp.where(picks(far_info, near + q), 1.0, 0.0).astype(bf16)
    far_factor = factors(far_info, near, experts + near)
    ftok_c.wait_recv()
    pack_tokens(chosen, far_tok, pack_tok, near)
    grad_send(near_grd, 0, 0)
    far_send(2)
    grad_send(near_grd, 0, 1)
    far_send(3)
    for c in loads[:2]:
        c.wait()
    for q in peers:
        tok_c[q].wait_recv()
    forward(0)

    def relay(t):
        fcot_c[t].wait_recv()
        pack_grads(chosen, far_factor, far_cot, pack_grd, near, t)
        grad_send(pack_grd, near, t)

    core_c, x_c = {}, {}

    def piece(j, t):
        part = pl.ds(pl.multiple_of(j * share, share), share)
        return jnp.dot(hid[part, :], grads[:, columns(t)], preferred_element_type=f32)

    def down_core(t):
        for d in (*peers, *(near + q for q in peers)):
            grd_c[d, t].wait_recv()
        core_out[2, :, columns(t)] = piece((1 - half) * 2 + (1 - side), t).astype(bf16)
        core_c[2, t] = pltpu.make_async_remote_copy(
            src_ref=core_out.at[2, :, columns(t)], dst_ref=core_in.at[2, :, columns(t)],
            send_sem=core_s.at[6 + t], recv_sem=core_r.at[6 + t],
            device_id={"dp": core_peer}, device_id_type=pl.DeviceIdType.MESH,
        )
        core_c[2, t].start()

    def down_x(t):
        v = piece((1 - half) * 2 + side, t)
        core_c[2, t].wait_recv()
        x_out[2, :, columns(t)] = (v + core_in[2, :, columns(t)].astype(f32)).astype(bf16)
        x_c[2, t] = pltpu.make_async_remote_copy(
            src_ref=x_out.at[2, :, columns(t)], dst_ref=x_in.at[2, :, columns(t)],
            send_sem=x_s.at[3 + t], recv_sem=x_r.at[3 + t],
            device_id={"dp": x_peer}, device_id_type=pl.DeviceIdType.MESH,
        )
        x_c[2, t].start()

    relay(0)
    grad_send(near_grd, 0, 2)
    grad_send(near_grd, 0, 3)
    relay(1)
    for q in peers:
        tok_c[near + q].wait_recv()
    forward(1)
    relay(2)
    down_core(0)
    relay(3)
    down_core(1)
    down_x(0)
    down_core(2)
    down_x(1)
    loads[2].wait()
    down_core(3)
    down_x(2)
    backward(0)
    backward(1)

    def send_core(k, a, j):
        def store(cols, v):
            core_out[k * 3 + a, :, cols] = v.astype(bf16)

        weight_grad(a, j, store)
        core_c[k, a] = pltpu.make_async_remote_copy(
            src_ref=core_out.at[k * 3 + a], dst_ref=core_in.at[k * 3 + a],
            send_sem=core_s.at[k * 3 + a], recv_sem=core_r.at[k * 3 + a],
            device_id={"dp": core_peer}, device_id_type=pl.DeviceIdType.MESH,
        )
        core_c[k, a].start()

    for a in range(2):
        send_core(0, a, (1 - half) * 2 + (1 - side))
    down_x(3)
    assign(0)
    own_back = pltpu.make_async_copy(dass.at[slots(0)], ret_ref.at[slots(0)], loc_sem.at[0])
    own_back.start()
    assign(1)
    for q in peers:
        ret_c[near + q] = to_expert(
            dass.at[slots(near + q)], relay_in.at[slots(q)], ret_s, ret_r, near + q, q
        )
    for q in peers:
        ret_c[q] = to_expert(dass.at[slots(q)], ret_ref.at[slots(q)], ret_s, ret_r, q, q)
    relay_in[slots(0), :] = dass[slots(near), :]
    for a in range(2):
        core_c[0, a].wait_recv()

        def store(cols, v, a=a):
            x_out[a, :, cols] = (v + core_in[a, :, cols].astype(f32)).astype(bf16)

        weight_grad(a, (1 - half) * 2 + side, store)
        x_c[a] = pltpu.make_async_remote_copy(
            src_ref=x_out.at[a], dst_ref=x_in.at[a], send_sem=x_s.at[a], recv_sem=x_r.at[a],
            device_id={"dp": x_peer}, device_id_type=pl.DeviceIdType.MESH,
        )
        x_c[a].start()
    for a in range(3):
        send_core(1, a, half * 2 + (1 - side))
    for q in peers:
        ret_c[near + q].wait_recv()

    @pl.loop(0, 4)
    def _(t):
        cols = pl.ds(pl.multiple_of(t * wide, wide), wide)
        v = lax.dot_general(chosen[...], relay_in[:, cols], TN, preferred_element_type=f32)
        part_out[:, cols] = v.astype(bf16)

    part_c = to_expert(part_out, part_in, far_s, far_r, 2, near)
    for a in range(3):
        core_c[1, a].wait_recv()

        def store(cols, v, a=a):
            own[a, :, cols] = v + core_in[3 + a, :, cols].astype(f32)

        weight_grad(a, half * 2 + side, store)
    for a, out in enumerate((og_ref, ou_ref, od_ref)):
        for key in [k for k in x_c if k == a or (a == 2 and isinstance(k, tuple))]:
            x_c[key].wait_recv()

        @pl.loop(0, 4)
        def _(t, a=a, out=out):
            cols = pl.ds(pl.multiple_of(t * wide, wide), wide)
            out[:, cols] = (own[a, :, cols] + x_in[a, :, cols].astype(f32)).astype(bf16)

    own_back.wait()
    for q in peers:
        ret_c[q].wait_recv()
    part_c.wait_recv()
    for c in (info_c, ftok_c, part_c, *fcot_c.values(), *grd_c.values()):
        c.wait_send()
    for d in tok_c:
        tok_c[d].wait_send()
        ret_c[d].wait_send()
    for c in core_c.values():
        c.wait_send()
    for c in x_c.values():
        c.wait_send()


def gathered(tokens, cotangent, routes, gates, gate_proj, up_proj, down_proj):
    experts = lax.axis_size("expert")
    tok_count, feature = tokens.shape
    chosen = routes.shape[1]
    ff = gate_proj.shape[1]
    capacity = max(2, min(tok_count, 5 * tok_count * chosen // (4 * experts)))
    cap = -(-capacity // 16) * 16
    f32, bf16 = jnp.float32, jnp.bfloat16
    near = experts // 2
    order = jnp.arange(experts, dtype=jnp.int32) ^ lax.axis_index("expert")
    hit = routes[:, :, None] == order[None, None, :]
    member = jnp.any(hit, axis=1)
    weight = jnp.sum(jnp.where(hit, gates[:, :, None], 0.0), axis=1)
    at = jnp.arange(tok_count, dtype=jnp.int32)
    earlier = (at[None, :] < at[:, None]).astype(bf16)
    slot = jnp.dot(earlier, member.astype(bf16), preferred_element_type=f32).astype(jnp.int32)
    slot = jnp.where(member, slot, cap)
    info = jnp.concatenate([slot.T.astype(f32), weight.T], axis=0)
    picks = slot.T[:near, None, :] == jnp.arange(cap, dtype=jnp.int32)[None, :, None]
    placing = picks.reshape(near * cap, tok_count).astype(bf16)
    group = experts * cap // 2
    share = ff // 4
    rows = experts * cap
    vm = pl.BlockSpec(memory_space=pltpu.VMEM)
    anyspec = pl.BlockSpec(memory_space=pl.ANY)
    sem = pltpu.SemaphoreType.DMA
    back, part, grad_gate, grad_up, grad_down = pl.pallas_call(
        functools.partial(layer_kernel, experts, cap, group),
        out_shape=[
            jax.ShapeDtypeStruct((near * cap, feature), bf16),
            jax.ShapeDtypeStruct((tok_count, feature), bf16),
        ]
        + [jax.ShapeDtypeStruct((share, feature), bf16)] * 3,
        in_specs=[vm, vm, vm, anyspec, anyspec, anyspec],
        out_specs=[vm] * 5,
        scratch_shapes=[
            pltpu.VMEM((rows, feature), bf16),
            pltpu.VMEM((rows, feature), bf16),
            pltpu.VMEM((ff, feature), bf16),
            pltpu.VMEM((ff, feature), bf16),
            pltpu.VMEM((ff, feature), bf16),
            pltpu.VMEM((ff, rows), f32),
            pltpu.VMEM((ff, rows), f32),
            pltpu.VMEM((ff, rows), bf16),
            pltpu.VMEM((ff, rows), bf16),
            pltpu.VMEM((ff, rows), bf16),
            pltpu.VMEM((rows, feature), bf16),
            pltpu.VMEM((tok_count, feature), bf16),
            pltpu.VMEM((tok_count, feature), bf16),
            pltpu.VMEM((2 * experts, tok_count), f32),
            pltpu.VMEM((near * cap, tok_count), bf16),
            pltpu.VMEM((near * cap, tok_count), bf16),
            pltpu.VMEM((near * cap, feature), bf16),
            pltpu.VMEM((near * cap, feature), bf16),
            pltpu.VMEM((near * cap, feature), bf16),
            pltpu.VMEM((near * cap, feature), bf16),
            pltpu.VMEM((near * cap, feature), bf16),
            pltpu.VMEM((tok_count, feature), bf16),
            pltpu.VMEM((6, share, feature), bf16),
            pltpu.VMEM((6, share, feature), bf16),
            pltpu.VMEM((3, share, feature), bf16),
            pltpu.VMEM((3, share, feature), bf16),
            pltpu.VMEM((3, share, feature), f32),
            sem((3,)), sem((1,)), sem((7,)), sem((7,)),
            sem((experts,)), sem((experts,)), sem((experts * 4,)), sem((experts * 4,)),
            sem((experts,)), sem((experts,)),
            sem((10,)), sem((10,)), sem((7,)), sem((7,)),
        ],
        compiler_params=pltpu.CompilerParams(
            collective_id=0, has_side_effects=True, vmem_limit_bytes=64 * 1024 * 1024 - 65536
        ),
    )(
        tokens, cotangent, info,
        gate_proj[0], up_proj[0], down_proj[0],
    )
    grad_tokens = lax.dot_general(placing, back, TN, preferred_element_type=f32)
    grad_tokens = (grad_tokens + part.astype(f32)).astype(bf16)
    return grad_tokens, grad_gate[None], grad_up[None], grad_down[None]


def fits(mesh):
    experts, replicas = mesh.shape["expert"], mesh.shape["dp"]
    return replicas == 4 and experts & (experts - 1) == 0 and experts <= 2 * replicas


def solution(mesh):
    return jax.shard_map(
        gathered if fits(mesh) else shards,
        mesh=mesh,
        in_specs=(
            P(("dp", "expert"), None),
            P(("dp", "expert"), None),
            P(("dp", "expert"), None),
            P(("dp", "expert"), None),
            P("expert", None, None),
            P("expert", None, None),
            P("expert", None, None),
        ),
        out_specs=(
            P(("dp", "expert"), None),
            P("expert", "dp", None),
            P("expert", "dp", None),
            P("expert", "dp", None),
        ),
        check_vma=False,
    )
```

```python
import functools

import jax
import jax.numpy as jnp
from jax import lax
from jax.experimental import pallas as pl
from jax.experimental.pallas import tpu as pltpu
from jax.sharding import PartitionSpec as P


def expert_pass(rows_in, rows_grad, w_gate, w_up, w_down):
    gate_pre = jnp.einsum("rd,fd->rf", rows_in, w_gate, preferred_element_type=jnp.float32)
    up_pre = jnp.einsum("rd,fd->rf", rows_in, w_up, preferred_element_type=jnp.float32)
    sigma = jax.nn.sigmoid(gate_pre)
    active = gate_pre * sigma
    hidden = (active * up_pre).astype(jnp.bfloat16)
    grad_down = jnp.einsum("rf,rd->fd", hidden, rows_grad, preferred_element_type=jnp.float32)
    d_hidden = jnp.einsum("rd,fd->rf", rows_grad, w_down, preferred_element_type=jnp.float32)
    d_up = (d_hidden * active).astype(jnp.bfloat16)
    d_gate = (d_hidden * up_pre * sigma * (1.0 + gate_pre * (1.0 - sigma))).astype(jnp.bfloat16)
    grad_gate = jnp.einsum("rf,rd->fd", d_gate, rows_in, preferred_element_type=jnp.float32)
    grad_up = jnp.einsum("rf,rd->fd", d_up, rows_in, preferred_element_type=jnp.float32)
    d_assign = jnp.dot(d_gate, w_gate, preferred_element_type=jnp.float32) + jnp.dot(
        d_up, w_up, preferred_element_type=jnp.float32
    )
    return (d_assign, grad_gate, grad_up, grad_down)


def shards(tokens, cotangent, routes, gates, gate_proj, up_proj, down_proj):
    experts = lax.axis_size("expert")
    tok_count = tokens.shape[0]
    feature = tokens.shape[1]
    chosen = routes.shape[1]
    capacity = max(2, min(tok_count, 5 * tok_count * chosen // (4 * experts)))
    routes_flat = routes.reshape(-1)
    onehot = (routes_flat[:, None] == jnp.arange(experts, dtype=jnp.int32)[None, :]).astype(
        jnp.int32
    )
    slot_index = jnp.sum((jnp.cumsum(onehot, axis=0) - onehot) * onehot, axis=1)
    target = routes_flat * capacity + slot_index
    placing = (jnp.arange(experts * capacity, dtype=jnp.int32)[:, None] == target[None, :]).astype(
        jnp.bfloat16
    )
    scaled = (
        gates.reshape(-1)[:, None] * jnp.repeat(cotangent, chosen, axis=0).astype(jnp.float32)
    ).astype(jnp.bfloat16)
    stacked = jnp.concatenate([jnp.repeat(tokens, chosen, axis=0), scaled], axis=1)
    packed = jnp.dot(placing, stacked, preferred_element_type=jnp.float32).astype(jnp.bfloat16)
    sent_tokens = packed[:, :feature].reshape(experts, capacity, feature)
    sent_grads = packed[:, feature:].reshape(experts, capacity, feature)
    arrived = (
        lax.all_to_all(sent_tokens, "expert", split_axis=0, concat_axis=0, tiled=True),
        lax.all_to_all(sent_grads, "expert", split_axis=0, concat_axis=0, tiled=True),
    )
    d_assign, whole_gate, whole_up, whole_down = expert_pass(
        arrived[0].reshape(-1, feature),
        arrived[1].reshape(-1, feature),
        gate_proj[0],
        up_proj[0],
        down_proj[0],
    )
    reduced = d_assign.reshape(experts, capacity, feature)
    grad_gate, grad_up, grad_down = (
        lax.psum_scatter(whole_gate, "dp", scatter_dimension=0, tiled=True),
        lax.psum_scatter(whole_up, "dp", scatter_dimension=0, tiled=True),
        lax.psum_scatter(whole_down, "dp", scatter_dimension=0, tiled=True),
    )
    summed = lax.all_to_all(reduced, "expert", split_axis=0, concat_axis=0, tiled=True)
    picked = jnp.take(summed.reshape(experts * capacity, feature), target, axis=0)
    grad_tokens = jnp.sum(picked.reshape(tok_count, chosen, feature), axis=1).astype(jnp.bfloat16)
    return (
        grad_tokens,
        grad_gate.astype(jnp.bfloat16)[None],
        grad_up.astype(jnp.bfloat16)[None],
        grad_down.astype(jnp.bfloat16)[None],
    )


NT = (((1,), (1,)), ((), ()))
TN = (((0,), (0,)), ((), ()))


def flip(index, offset, count):
    total, bit = 0, 1
    while bit < count:
        total = total + ((index // bit) % 2 + (offset // bit) % 2) % 2 * bit
        bit *= 2
    return total


def layer_kernel(
    experts, cap, group, all_tok, all_cot, info_ref, wg_hbm, wu_hbm, wd_hbm,
    ot_ref, og_ref, ou_ref, od_ref,
    rows, grads, wg, wu, wd, gate, up, hid, dgate, dup, dass,
    far_tok, far_cot, far_info, chosen, mine, near_tok, near_grd, pack_tok, pack_grd, relay_in, part_out, ret_ref, part_in,
    core_out, core_in, x_out, x_in, own,
    w_sem, loc_sem, far_s, far_r, tok_s, tok_r, grd_s, grd_r, ret_s, ret_r, core_s, core_r, x_s, x_r,
):
    me = lax.axis_index("expert")
    rank = lax.axis_index("dp")
    half, side = rank // 2, rank % 2
    core_peer = half * 2 + (1 - side)
    x_peer = (1 - half) * 2 + side
    ff, feature = wg.shape
    share = ff // 4
    f32, bf16 = jnp.float32, jnp.bfloat16

    loads = [
        pltpu.make_async_copy(a, b, w_sem.at[i])
        for i, (a, b) in enumerate(((wg_hbm, wg), (wu_hbm, wu), (wd_hbm, wd)))
    ]
    for c in loads:
        c.start()
    barrier = pltpu.get_barrier_semaphore()
    near = experts // 2
    peers = list(range(1, near))
    for d in peers + [near]:
        pl.semaphore_signal(barrier, inc=1, device_id={"expert": flip(me, d, experts)}, device_id_type=pl.DeviceIdType.MESH)
    for p in (core_peer, x_peer):
        pl.semaphore_signal(barrier, inc=1, device_id={"dp": p}, device_id_type=pl.DeviceIdType.MESH)
    pl.semaphore_wait(barrier, near + 2)

    def to_expert(src, dst, s, r, at, d):
        copy = pltpu.make_async_remote_copy(
            src_ref=src, dst_ref=dst, send_sem=s.at[at], recv_sem=r.at[at],
            device_id={"expert": flip(me, d, experts)}, device_id_type=pl.DeviceIdType.MESH,
        )
        copy.start()
        return copy

    def slots(d):
        return pl.ds(d * cap, cap)

    tok_c, grd_c, ret_c, fcot_c = {}, {}, {}, {}
    count = all_tok.shape[0]
    wide = feature // 4
    steps = range(4)

    def columns(t):
        return pl.ds(t * wide, wide)

    def picks(table, q):
        place = lax.broadcasted_iota(jnp.int32, (cap, count), 0).astype(f32)
        return place == table[q : q + 1, :]

    def factors(table, first, weights):
        return jnp.concatenate(
            [
                jnp.sum(
                    jnp.where(picks(table, first + q), table[weights + q : weights + q + 1, :], 0.0),
                    axis=1,
                    keepdims=True,
                )
                for q in range(near)
            ],
            axis=0,
        )

    def far_send(t):
        fcot_c[t] = to_expert(
            all_cot.at[:, columns(t)], far_cot.at[:, columns(t)], far_s, far_r, 3 + t, near
        )

    def grad_send(source, base, t):
        for q in peers:
            grd_c[base + q, t] = to_expert(
                source.at[slots(q), columns(t)], grads.at[slots(base + q), columns(t)],
                grd_s, grd_r, (base + q) * 4 + t, q,
            )

    def pack_grads(sel, factor, source, out, base, t):
        v = jnp.dot(sel[...], source[:, columns(t)], preferred_element_type=f32)
        v = (factor * v).astype(bf16)
        out[:, columns(t)] = v
        grads[slots(base), columns(t)] = v[:cap]

    def pack_tokens(sel, source, out, base):
        for t in steps:
            v = jnp.dot(sel[...], source[:, columns(t)], preferred_element_type=f32).astype(bf16)
            out[:, columns(t)] = v
            rows[slots(base), columns(t)] = v[:cap]
        for q in peers:
            tok_c[base + q] = to_expert(
                out.at[slots(q)], rows.at[slots(base + q)], tok_s, tok_r, base + q, q
            )

    info_c = to_expert(info_ref, far_info, far_s, far_r, 0, near)
    ftok_c = to_expert(all_tok, far_tok, far_s, far_r, 1, near)
    for q in range(near):
        mine[slots(q), :] = jnp.where(picks(info_ref, q), 1.0, 0.0).astype(bf16)
    pack_tokens(mine, all_tok, near_tok, 0)
    far_send(0)
    far_send(1)
    near_factor = factors(info_ref, 0, experts)
    for t in steps:
        pack_grads(mine, near_factor, all_cot, near_grd, 0, t)

    tile = ff // 2

    def forward(g):
        span = pl.ds(g * group, group)

        @pl.loop(0, 2)
        def _(t):
            part = pl.ds(pl.multiple_of(t * tile, tile), tile)
            x = rows[span, :]
            gp = lax.dot_general(wg[part, :], x, NT, preferred_element_type=f32)
            u = lax.dot_general(wu[part, :], x, NT, preferred_element_type=f32)
            gate[part, span] = gp
            up[part, span] = u
            hid[part, span] = (gp * jax.nn.sigmoid(gp) * u).astype(bf16)

    def backward(g):
        span = pl.ds(g * group, group)

        @pl.loop(0, 2)
        def _(t):
            part = pl.ds(pl.multiple_of(t * tile, tile), tile)
            dh = lax.dot_general(wd[part, :], grads[span, :], NT, preferred_element_type=f32)
            gp = gate[part, span]
            s = jax.nn.sigmoid(gp)
            dup[part, span] = (dh * (gp * s)).astype(bf16)
            dgate[part, span] = (dh * up[part, span] * s * (1.0 + gp * (1.0 - s))).astype(bf16)

    def assign(g):
        span = pl.ds(g * group, group)

        @pl.loop(0, 4)
        def _(t):
            cols = pl.ds(pl.multiple_of(t * wide, wide), wide)
            v = lax.dot_general(dgate[:, span], wg[:, cols], TN, preferred_element_type=f32)
            v += lax.dot_general(dup[:, span], wu[:, cols], TN, preferred_element_type=f32)
            dass[span, cols] = v.astype(bf16)

    def weight_grad(a, j, store):
        left = (dgate, dup, hid)[a]
        right = (rows, rows, grads)[a]
        part = pl.ds(pl.multiple_of(j * share, share), share)

        @pl.loop(0, 4)
        def _(t):
            cols = pl.ds(pl.multiple_of(t * wide, wide), wide)
            store(cols, jnp.dot(left[part, :], right[:, cols], preferred_element_type=f32))

    info_c.wait_recv()
    for q in range(near):
        chosen[slots(q), :] = jnp.where(picks(far_info, near + q), 1.0, 0.0).astype(bf16)
    far_factor = factors(far_info, near, experts + near)
    ftok_c.wait_recv()
    pack_tokens(chosen, far_tok, pack_tok, near)
    grad_send(near_grd, 0, 0)
    far_send(2)
    grad_send(near_grd, 0, 1)
    far_send(3)
    for c in loads[:2]:
        c.wait()
    for q in peers:
        tok_c[q].wait_recv()
    forward(0)

    def relay(t):
        fcot_c[t].wait_recv()
        pack_grads(chosen, far_factor, far_cot, pack_grd, near, t)
        grad_send(pack_grd, near, t)

    core_c, x_c = {}, {}

    def piece(j, t):
        part = pl.ds(pl.multiple_of(j * share, share), share)
        return jnp.dot(hid[part, :], grads[:, columns(t)], preferred_element_type=f32)

    def down_core(t):
        for q in peers:
            grd_c[near + q, t].wait_recv()
        core_out[2, :, columns(t)] = piece((1 - half) * 2 + (1 - side), t).astype(bf16)
        core_c[2, t] = pltpu.make_async_remote_copy(
            src_ref=core_out.at[2, :, columns(t)], dst_ref=core_in.at[2, :, columns(t)],
            send_sem=core_s.at[6 + t], recv_sem=core_r.at[6 + t],
            device_id={"dp": core_peer}, device_id_type=pl.DeviceIdType.MESH,
        )
        core_c[2, t].start()

    def down_x(t):
        v = piece((1 - half) * 2 + side, t)
        core_c[2, t].wait_recv()
        x_out[2, :, columns(t)] = (v + core_in[2, :, columns(t)].astype(f32)).astype(bf16)
        x_c[2, t] = pltpu.make_async_remote_copy(
            src_ref=x_out.at[2, :, columns(t)], dst_ref=x_in.at[2, :, columns(t)],
            send_sem=x_s.at[3 + t], recv_sem=x_r.at[3 + t],
            device_id={"dp": x_peer}, device_id_type=pl.DeviceIdType.MESH,
        )
        x_c[2, t].start()

    relay(0)
    grad_send(near_grd, 0, 2)
    grad_send(near_grd, 0, 3)
    relay(1)
    for q in peers:
        tok_c[near + q].wait_recv()
    forward(1)
    relay(2)
    for q in peers:
        for t in steps:
            grd_c[q, t].wait_recv()
    down_core(0)
    relay(3)
    down_core(1)
    down_x(0)
    loads[2].wait()
    backward(0)
    down_core(2)
    down_x(1)
    down_core(3)
    backward(1)

    def send_core(k, a, j):
        def store(cols, v):
            core_out[k * 3 + a, :, cols] = v.astype(bf16)

        weight_grad(a, j, store)
        core_c[k, a] = pltpu.make_async_remote_copy(
            src_ref=core_out.at[k * 3 + a], dst_ref=core_in.at[k * 3 + a],
            send_sem=core_s.at[k * 3 + a], recv_sem=core_r.at[k * 3 + a],
            device_id={"dp": core_peer}, device_id_type=pl.DeviceIdType.MESH,
        )
        core_c[k, a].start()

    for a in range(2):
        send_core(0, a, (1 - half) * 2 + (1 - side))
    down_x(2)
    down_x(3)
    assign(0)
    own_back = pltpu.make_async_copy(dass.at[slots(0)], ret_ref.at[slots(0)], loc_sem.at[0])
    own_back.start()
    assign(1)
    for q in peers:
        ret_c[near + q] = to_expert(
            dass.at[slots(near + q)], relay_in.at[slots(q)], ret_s, ret_r, near + q, q
        )
    for q in peers:
        ret_c[q] = to_expert(dass.at[slots(q)], ret_ref.at[slots(q)], ret_s, ret_r, q, q)
    relay_in[slots(0), :] = dass[slots(near), :]
    for a in range(2):
        core_c[0, a].wait_recv()

        def store(cols, v, a=a):
            x_out[a, :, cols] = (v + core_in[a, :, cols].astype(f32)).astype(bf16)

        weight_grad(a, (1 - half) * 2 + side, store)
        x_c[a] = pltpu.make_async_remote_copy(
            src_ref=x_out.at[a], dst_ref=x_in.at[a], send_sem=x_s.at[a], recv_sem=x_r.at[a],
            device_id={"dp": x_peer}, device_id_type=pl.DeviceIdType.MESH,
        )
        x_c[a].start()
    for a in range(3):
        send_core(1, a, half * 2 + (1 - side))
    for q in peers:
        ret_c[near + q].wait_recv()

    @pl.loop(0, 4)
    def _(t):
        cols = pl.ds(pl.multiple_of(t * wide, wide), wide)
        v = lax.dot_general(chosen[...], relay_in[:, cols], TN, preferred_element_type=f32)
        part_out[:, cols] = v.astype(bf16)

    part_c = to_expert(part_out, part_in, far_s, far_r, 2, near)
    for a in range(3):
        core_c[1, a].wait_recv()

        def store(cols, v, a=a):
            own[a, :, cols] = v + core_in[3 + a, :, cols].astype(f32)

        weight_grad(a, half * 2 + side, store)
    own_back.wait()
    for q in peers:
        ret_c[q].wait_recv()
    part_c.wait_recv()

    @pl.loop(0, 4)
    def _(t):
        cols = pl.ds(pl.multiple_of(t * wide, wide), wide)
        v = lax.dot_general(mine[...], ret_ref[:, cols], TN, preferred_element_type=f32)
        ot_ref[:, cols] = (v + part_in[:, cols].astype(f32)).astype(bf16)

    for a, out in enumerate((og_ref, ou_ref, od_ref)):
        for key in [k for k in x_c if k == a or (a == 2 and isinstance(k, tuple))]:
            x_c[key].wait_recv()

        @pl.loop(0, 4)
        def _(t, a=a, out=out):
            cols = pl.ds(pl.multiple_of(t * wide, wide), wide)
            out[:, cols] = (own[a, :, cols] + x_in[a, :, cols].astype(f32)).astype(bf16)

    for c in (info_c, ftok_c, part_c, *fcot_c.values(), *grd_c.values()):
        c.wait_send()
    for d in tok_c:
        tok_c[d].wait_send()
        ret_c[d].wait_send()
    for c in core_c.values():
        c.wait_send()
    for c in x_c.values():
        c.wait_send()


def gathered(tokens, cotangent, routes, gates, gate_proj, up_proj, down_proj):
    experts = lax.axis_size("expert")
    tok_count, feature = tokens.shape
    chosen = routes.shape[1]
    ff = gate_proj.shape[1]
    capacity = max(2, min(tok_count, 5 * tok_count * chosen // (4 * experts)))
    cap = -(-capacity // 16) * 16
    f32, bf16 = jnp.float32, jnp.bfloat16
    near = experts // 2
    order = jnp.arange(experts, dtype=jnp.int32) ^ lax.axis_index("expert")
    hit = routes[:, :, None] == order[None, None, :]
    member = jnp.any(hit, axis=1)
    weight = jnp.sum(jnp.where(hit, gates[:, :, None], 0.0), axis=1)
    at = jnp.arange(tok_count, dtype=jnp.int32)
    earlier = (at[None, :] < at[:, None]).astype(bf16)
    slot = jnp.dot(earlier, member.astype(bf16), preferred_element_type=f32).astype(jnp.int32)
    slot = jnp.where(member, slot, cap)
    info = jnp.concatenate([slot.T.astype(f32), weight.T], axis=0)
    group = experts * cap // 2
    share = ff // 4
    rows = experts * cap
    vm = pl.BlockSpec(memory_space=pltpu.VMEM)
    anyspec = pl.BlockSpec(memory_space=pl.ANY)
    sem = pltpu.SemaphoreType.DMA
    grad_tokens, grad_gate, grad_up, grad_down = pl.pallas_call(
        functools.partial(layer_kernel, experts, cap, group),
        out_shape=[
            jax.ShapeDtypeStruct((tok_count, feature), bf16),
        ]
        + [jax.ShapeDtypeStruct((share, feature), bf16)] * 3,
        in_specs=[vm, vm, vm, anyspec, anyspec, anyspec],
        out_specs=[vm] * 4,
        scratch_shapes=[
            pltpu.VMEM((rows, feature), bf16),
            pltpu.VMEM((rows, feature), bf16),
            pltpu.VMEM((ff, feature), bf16),
            pltpu.VMEM((ff, feature), bf16),
            pltpu.VMEM((ff, feature), bf16),
            pltpu.VMEM((ff, rows), f32),
            pltpu.VMEM((ff, rows), f32),
            pltpu.VMEM((ff, rows), bf16),
            pltpu.VMEM((ff, rows), bf16),
            pltpu.VMEM((ff, rows), bf16),
            pltpu.VMEM((rows, feature), bf16),
            pltpu.VMEM((tok_count, feature), bf16),
            pltpu.VMEM((tok_count, feature), bf16),
            pltpu.VMEM((2 * experts, tok_count), f32),
            pltpu.VMEM((near * cap, tok_count), bf16),
            pltpu.VMEM((near * cap, tok_count), bf16),
            pltpu.VMEM((near * cap, feature), bf16),
            pltpu.VMEM((near * cap, feature), bf16),
            pltpu.VMEM((near * cap, feature), bf16),
            pltpu.VMEM((near * cap, feature), bf16),
            pltpu.VMEM((near * cap, feature), bf16),
            pltpu.VMEM((tok_count, feature), bf16),
            pltpu.VMEM((near * cap, feature), bf16),
            pltpu.VMEM((tok_count, feature), bf16),
            pltpu.VMEM((6, share, feature), bf16),
            pltpu.VMEM((6, share, feature), bf16),
            pltpu.VMEM((3, share, feature), bf16),
            pltpu.VMEM((3, share, feature), bf16),
            pltpu.VMEM((3, share, feature), f32),
            sem((3,)), sem((1,)), sem((7,)), sem((7,)),
            sem((experts,)), sem((experts,)), sem((experts * 4,)), sem((experts * 4,)),
            sem((experts,)), sem((experts,)),
            sem((10,)), sem((10,)), sem((7,)), sem((7,)),
        ],
        compiler_params=pltpu.CompilerParams(
            collective_id=0, has_side_effects=True, vmem_limit_bytes=64 * 1024 * 1024 - 65536
        ),
    )(
        tokens, cotangent, info,
        gate_proj[0], up_proj[0], down_proj[0],
    )
    return grad_tokens, grad_gate[None], grad_up[None], grad_down[None]


def fits(mesh):
    experts, replicas = mesh.shape["expert"], mesh.shape["dp"]
    return replicas == 4 and experts & (experts - 1) == 0 and experts <= 2 * replicas


def solution(mesh):
    return jax.shard_map(
        gathered if fits(mesh) else shards,
        mesh=mesh,
        in_specs=(
            P(("dp", "expert"), None),
            P(("dp", "expert"), None),
            P(("dp", "expert"), None),
            P(("dp", "expert"), None),
            P("expert", None, None),
            P("expert", None, None),
            P("expert", None, None),
        ),
        out_specs=(
            P(("dp", "expert"), None),
            P("expert", "dp", None),
            P("expert", "dp", None),
            P("expert", "dp", None),
        ),
        check_vma=False,
    )
```
